768 devices in a mesh: ma: 48 (over x, z_lo, core), row: 16 (over z_hi, y).
Axes of the slice: x: 4, y: 8, z: 12 (z_hi: 2, z_lo: 6; z = z_hi * 6 + z_lo), core: 2. Of those that a mesh axis runs over, the one named last changes fastest.
Arguments:
- velocity: bfloat16 [3, 2, 384, 128, 384], P(None, None, 'ma', 'row'), may hold values from -6 to 6
- vorticity: bfloat16 [3, 2, 384, 128, 384], P(None, None, 'ma', 'row'), may hold values from -6 to 6
- order_table: int32 [384], replicated, may hold values from 0 to 383, as said below
- legendre_bf: bfloat16 [384, 384, 576], P('ma'), may hold values from -24 to 24, as said below
- weighted: bfloat16 [384, 384, 576], P('ma'), may hold values from -1 to 1, as said below
- inverse_operators: float32 [384, 128, 128], P('row'), may hold values from -1.5 to 1.5
Outputs:
- advanced: float32 [3, 2, 384, 384, 128], P(None, None, 'ma', 'row')
The draws below stay inside these ranges and needn't reach their ends.
Inputs may be any that keep to these rules, and one draw needn't show every extreme that they name: `order_table`: slots 2k and 2k + 1 hold wavenumbers that add up to 383, and every wavenumber from 0 to 383 stands in exactly one slot. legendre_bf[slot, l, j] is Pbar_l^m(x_j) rounded to bfloat16, with m = order_table[slot], x_j = cos(pi (j + 0.5) / 576), s_j = sin(pi (j + 0.5) / 576), zero for l < m, Pbar_m^m = exp(-0.5 log 2 + 0.5 (lgamma(m + 1.5) - lgamma(m + 1) - lgamma(1.5)) + m log s_j) and Pbar_l^m = a (x_j Pbar_(l-1)^m - b Pbar_(l-2)^m), a = sqrt((4 l^2 - 1) / (l^2 - m^2)), b = sqrt(((l - 1)^2 - m^2) / (4 (l - 1)^2 - 1)). weighted[slot, l, j] is w_j Pbar_l^m(x_j), computed in float32 and rounded to bfloat16, with w_j = pi s_j / 576.
All inputs are finite; a program needn't handle non-finite values.
Results may differ from the reference program's by a relative error of at most 0.005.
Values may be sent and summed in bfloat16 or wider, within the bound.
No kernel may reach another device: no remote copies, remote signals or barrier semaphores. Data moves between devices by JAX's collectives and lax.ppermute only.
A program may use at most 64 MiB of HBM per device.

```python
import math
import jax
import jax.numpy as jnp
from jax import lax

NL = 384
NLAT = 576
NLON = 1152
NR = 128
NM = 384
N_MA = 48


rescale_limit = 10000000000.0


rescale_log = 23.025850929940457


gamma_offset = 0.06039111881762261


def order_pairs(key):
    pair_low = jax.random.permutation(jax.random.fold_in(key, 11), NL // 2).astype(jnp.int32)
    return jnp.stack([pair_low, NL - 1 - pair_low], axis=1).reshape(NL).astype(jnp.int32)


def legendre_values(key):
    orders = order_pairs(key)
    angles = (jnp.arange(NLAT, dtype=jnp.float32) + 0.5) * (math.pi / NLAT)
    cosines = jnp.cos(angles)
    sine_values = jnp.sin(angles)
    order_value = orders.astype(jnp.float32)[:, None]
    order_index = orders.astype(jnp.int32)[:, None]
    order_square = order_value * order_value
    log_start = -0.5 * math.log(2.0) + gamma_offset + 0.5 * (lax.lgamma(order_value + 1.5) - lax.lgamma(order_value + 1.0)) + order_value * jnp.log(sine_values)[None, :]
    cosine_row = cosines[None, :]
    start_zero = jnp.zeros(log_start.shape, jnp.float32)
    start_one = jnp.ones(log_start.shape, jnp.float32)

    def advance(carried, degree):
        earlier, current, log_scale = carried
        degree_value = degree.astype(jnp.float32)
        lower_degree = degree_value - 1.0
        moving = degree > order_index
        factor_up = jnp.sqrt(jnp.maximum(4.0 * degree_value * degree_value - 1.0, 1.0) / jnp.maximum(degree_value * degree_value - order_square, 1.0))
        factor_back = jnp.sqrt(jnp.maximum(lower_degree * lower_degree - order_square, 0.0) / jnp.maximum(4.0 * lower_degree * lower_degree - 1.0, 1.0))
        updated = factor_up * (cosine_row * current - factor_back * earlier)
        following = jnp.where(moving, updated, current)
        previous = jnp.where(moving, current, earlier)
        too_large = jnp.abs(following) > rescale_limit
        following = jnp.where(too_large, following / rescale_limit, following)
        previous = jnp.where(too_large, previous / rescale_limit, previous)
        log_scale = jnp.where(too_large, log_scale + rescale_log, log_scale)
        emitted = jnp.where(degree >= order_index, following * jnp.exp(log_scale), 0.0)
        return ((previous, following, log_scale), emitted)
    degree_list = jnp.arange(NL, dtype=jnp.int32)
    final_state, values = lax.scan(advance, (start_zero, start_one, log_start), degree_list)
    return (jnp.transpose(values, (1, 0, 2)), sine_values)


def draw_order_table(key, part):
    return order_pairs(key)


def draw_legendre_bf(key, part):
    values, sine_values = legendre_values(key)
    return values.astype(jnp.bfloat16)


def draw_weighted(key, part):
    values, sine_values = legendre_values(key)
    quad_weights = sine_values * (math.pi / NLAT)
    return (values * quad_weights[None, None, :]).astype(jnp.bfloat16)


def draw_inverse_operators(key, part):
    key_diag = jax.random.fold_in(key, 21)
    key_coupling = jax.random.fold_in(key, 22)
    diagonal = jax.random.uniform(key_diag, (NL, NR), jnp.float32, 0.5, 1.0)
    coupling = jax.random.normal(key_coupling, (NL, NR, NR), jnp.float32)
    identity = jnp.eye(NR, dtype=jnp.float32)
    return coupling * (0.6 / math.sqrt(NR)) + identity[None, :, :] * diagonal[:, :, None]


def block_levels(rng, extent, cuts, smallest, top_value):
    level, own = 1.0, jax.random.fold_in(rng, 6)
    for dim, parts in cuts:
        draws = jnp.exp(jax.random.uniform(jax.random.fold_in(own, dim), (parts,), jnp.float32, smallest / len(cuts), top_value / len(cuts)))
        level = level * jnp.repeat(draws, extent[dim] // parts).reshape([-1 if axis == dim else 1 for axis in range(len(extent))])
    return level


def scatter_about(key, shape, scale, reach, cuts=(), kind=jnp.bfloat16):
    drawn = scale * jax.random.normal(key, shape, jnp.float32)
    if cuts:
        drawn = drawn * block_levels(key, shape, cuts, -0.22, 0.18)
    return jnp.clip(drawn, -reach, reach).astype(kind)


def setup_inputs(seed: int = 0) -> dict:
    keys = jax.random.split(jax.random.key(seed), 7)
    return {
        "velocity": scatter_about(keys[0], (3, 2, NM, NR, NL), 1.0, 6.0, ((2, 48), (3, 16))),
        "vorticity": scatter_about(keys[1], (3, 2, NM, NR, NL), 1.0, 6.0, ((2, 48), (3, 16))),
        "order_table": draw_order_table(jax.random.fold_in(keys[6], 71), 0),
        "legendre_bf": draw_legendre_bf(jax.random.fold_in(keys[6], 71), 0),
        "weighted": draw_weighted(jax.random.fold_in(keys[6], 71), 0),
        "inverse_operators": draw_inverse_operators(jax.random.fold_in(keys[6], 71), 0),
    }


time_step = 0.5
rotation = 2.0


def longitude_table(orders):
    points = jnp.arange(NLON, dtype=jnp.int32)
    phases = (orders.astype(jnp.int32)[:, None] * points[None, :]) % NLON
    angles = phases.astype(jnp.float32) * (2.0 * math.pi / NLON)
    return jnp.stack([jnp.cos(angles), -jnp.sin(angles)]).astype(jnp.bfloat16)


def cross_terms(moving, spinning):
    spin_total = spinning[2] + rotation
    component_one = moving[1] * spin_total - moving[2] * spinning[1]
    component_two = moving[2] * spinning[0] - moving[0] * spin_total
    component_three = moving[0] * spinning[1] - moving[1] * spinning[0]
    return jnp.stack([component_one, component_two, component_three])


def reference(velocity, vorticity, order_table, legendre_bf, weighted, inverse_operators):
    highest = lax.Precision.HIGHEST
    slot_block = NM // N_MA
    lat_block = NLAT // N_MA
    spectral = jnp.concatenate([velocity, vorticity], axis=0)
    spec_blocks = spectral.reshape(6, 2, N_MA, slot_block, NR, NL).transpose(2, 0, 1, 3, 4, 5)
    table_blocks = legendre_bf.reshape(N_MA, slot_block, NL, NLAT)
    weight_blocks = weighted.reshape(N_MA, slot_block, NL, NLAT)
    slot_scale = jnp.where(order_table == 0, 1.0, 2.0).astype(jnp.float32) / NL
    scale_blocks = slot_scale.reshape(N_MA, slot_block)

    def synthesize(pieces):
        block_spec, block_table, block_scale = pieces
        grid_values = jnp.einsum('cpsrl,slt->cpsrt', block_spec.astype(jnp.float32),
                                 block_table.astype(jnp.float32), precision=highest)
        return (grid_values * block_scale[None, None, :, None, None]).astype(jnp.bfloat16)

    grid_blocks = lax.map(synthesize, (spec_blocks, table_blocks, scale_blocks))
    grid_spec = grid_blocks.transpose(1, 2, 0, 3, 4, 5).reshape(6, 2, NM, NR, NLAT)
    harmonics = longitude_table(order_table).astype(jnp.float32)
    lat_pieces = grid_spec.reshape(6, 2, NM, NR, N_MA, lat_block).transpose(4, 0, 1, 2, 3, 5)

    def nonlinear(lat_piece):
        grid_values = jnp.einsum('cpsrt,psn->crtn', lat_piece.astype(jnp.float32),
                                 harmonics, precision=highest)
        products = cross_terms(grid_values[:3], grid_values[3:]).astype(jnp.bfloat16)
        spectral_back = jnp.einsum('crtn,psn->cpsrt', products.astype(jnp.float32),
                                   harmonics, precision=highest)
        return ((NL / NLON) * spectral_back).astype(jnp.bfloat16)

    gathered_terms = lax.map(nonlinear, lat_pieces)
    tendency_grid = gathered_terms.transpose(1, 2, 3, 4, 0, 5).reshape(3, 2, NM, NR, NLAT)
    tend_blocks = tendency_grid.reshape(3, 2, N_MA, slot_block, NR, NLAT).transpose(2, 0, 1, 3, 4, 5)

    def analyze(pieces):
        block_terms, block_weights = pieces
        return jnp.einsum('cpsrt,slt->cpsrl', block_terms.astype(jnp.float32),
                          block_weights.astype(jnp.float32), precision=highest)

    term_blocks = lax.map(analyze, (tend_blocks, weight_blocks))
    spec_terms = term_blocks.transpose(1, 2, 0, 3, 4, 5).reshape(3, 2, NM, NR, NL)
    right_side = velocity.astype(jnp.float32) + time_step * spec_terms
    return jnp.einsum('lab,cpsbl->cpsla', inverse_operators, right_side, precision=highest)
```

```python
import functools
import math

import jax
import jax.numpy as jnp
from jax import lax
from jax.experimental import pallas as pl
from jax.experimental.pallas import tpu as pltpu
from jax.sharding import PartitionSpec as P

NL = 384
NLAT = 576
NLON = 1152
NR = 128
LANES = 128


time_step = 0.5
rotation = 2.0

NT_DIMS = (((1,), (1,)), ((), ()))


def dot(left, right, dims=(((1,), (0,)), ((), ()))):
    return lax.dot_general(left, right, dims, preferred_element_type=jnp.float32)


def angle_parts(orders, steps):
    phases = orders[:, None] * steps[None, :] % NLON
    angles = phases.astype(jnp.float32) * (2.0 * math.pi / NLON)
    return jnp.cos(angles), jnp.sin(angles)


def harmonics_kernel(coarse_cos, coarse_sin, fine_cos, fine_sin, table):
    cos_b = fine_cos[...]
    sin_b = fine_sin[...]
    for block in range(NLON // LANES):
        cos_a = coarse_cos[:, block : block + 1]
        sin_a = coarse_sin[:, block : block + 1]
        lanes = pl.ds(block * LANES, LANES)
        table[0, :, lanes] = (cos_a * cos_b - sin_a * sin_b).astype(jnp.bfloat16)
        table[1, :, lanes] = (-(sin_a * cos_b + cos_a * sin_b)).astype(jnp.bfloat16)


def synthesis_kernel(groups, width, orders, velocity, vorticity, legendre, out, stage, rows, blocks):
    slot = pl.program_id(0)
    radii = velocity.shape[1]
    slots = orders.shape[0]
    own = jnp.where(orders[slot] == 0, 1.0, 2.0).astype(jnp.float32) / NL
    for index, field in enumerate((velocity, vorticity)):
        half = field.shape[0] * radii
        spectral = field[...].astype(jnp.float32).reshape(half, NL).astype(jnp.bfloat16)
        stage[index * half : (index + 1) * half, :] = dot(spectral, legendre[0], NT_DIMS) * own
    for group in range(groups):
        for component in range(6):
            for part in range(2):
                source = (component * 2 + part) * radii
                target = (part * 6 + component) * width
                rows[group, :, target : target + width] = stage[
                    source : source + radii, group * width : (group + 1) * width
                ]
        for tile in range(blocks.shape[0]):
            lanes = slice(tile * LANES, (tile + 1) * LANES)
            blocks[tile, pl.ds(group * radii * slots + slot, radii, stride=slots), :] = rows[group, :, lanes]

    @pl.when(slot == slots - 1)
    def finish():
        for tile in range(blocks.shape[0]):
            out[:, tile * LANES : (tile + 1) * LANES] = blocks[tile].astype(jnp.bfloat16)


def longitude_kernel(width, received, table, out, stage):
    points = 6 * width
    turned = received[...].astype(jnp.float32).T.astype(jnp.bfloat16)
    grid = dot(turned[:points], table[0]) + dot(turned[points:], table[1])
    u = [grid[c * width : (c + 1) * width] for c in range(3)]
    w = [grid[(3 + c) * width : (4 + c) * width] for c in range(3)]
    spin = w[2] + rotation
    products = jnp.concatenate(
        [
            u[1] * spin - u[2] * w[1],
            u[2] * w[0] - u[0] * spin,
            u[0] * w[1] - u[1] * w[0],
        ],
        axis=0,
    ).astype(jnp.bfloat16)
    for part in range(2):
        back = dot(table[part], products, NT_DIMS) * (NL / NLON)
        stage[:, part * 3 * width : (part + 1) * 3 * width] = back
    out[...] = stage[...].astype(jnp.bfloat16)


def analysis_kernel(groups, width, degrees, received, velocity, weighted, out, whole, rows, stage, side, blocks):
    slots = weighted.shape[0]
    radii = velocity.shape[2]
    owners = NL // degrees
    lanes = 6 * width
    for tile in range(whole.shape[0]):
        size = min(LANES, lanes - tile * LANES)
        whole[tile, :, :size] = received[:, tile * LANES : tile * LANES + size].astype(jnp.float32)
    for slot in range(slots):
        for group in range(groups):
            for tile in range(whole.shape[0]):
                rows[slot, group, :, tile * LANES : (tile + 1) * LANES] = whole[
                    tile, pl.ds(group * radii * slots + slot, radii, stride=slots), :
                ]
            for component in range(3):
                for part in range(2):
                    source = (part * 3 + component) * width
                    target = (component * 2 + part) * radii
                    stage[slot, target : target + radii, group * width : (group + 1) * width] = rows[
                        slot, group, :, source : source + width
                    ]
        terms = dot(stage[slot].astype(jnp.bfloat16), weighted[slot])
        known = velocity[:, slot].astype(jnp.float32).reshape(6 * radii, NL)
        side[slot] = known + time_step * terms
        for owner in range(owners):
            for field in range(6):
                target = (field * slots + slot) * degrees
                blocks[owner * radii : (owner + 1) * radii, target : target + degrees] = side[
                    slot, field * radii : (field + 1) * radii, owner * degrees : (owner + 1) * degrees
                ]
    out[...] = blocks[...].astype(jnp.bfloat16)


def solve_kernel(received, operators, out, turned):
    degrees = operators.shape[0]
    count = received.shape[1] // degrees
    turned[...] = received[...].astype(jnp.float32).T
    for degree in range(degrees):
        rows = turned[pl.ds(degree, count, stride=degrees), :].astype(jnp.bfloat16)
        operator = operators[degree]
        high = operator.astype(jnp.bfloat16)
        low = (operator - high.astype(jnp.float32)).astype(jnp.bfloat16)
        out[pl.ds(degree, count, stride=degrees), :] = dot(rows, high, NT_DIMS) + dot(rows, low, NT_DIMS)


def per_device(velocity, vorticity, order_table, legendre_bf, weighted, inverse_operators):
    slots = velocity.shape[2]
    radii = velocity.shape[3]
    degrees = inverse_operators.shape[0]
    members = NL // slots
    owners = NL // degrees
    groups = members // radii
    width = NLAT // groups
    f32, bf16 = jnp.float32, jnp.bfloat16
    vmem = pl.BlockSpec(memory_space=pltpu.VMEM)

    own_orders = lax.dynamic_slice_in_dim(order_table, lax.axis_index("ma") * slots, slots)
    velocity_rows = velocity.reshape(6, slots, radii, NL)
    vorticity_rows = vorticity.reshape(6, slots, radii, NL)
    legendre_rows = jnp.swapaxes(legendre_bf, 1, 2)
    weighted_rows = jnp.swapaxes(weighted, 1, 2)

    field_spec = pl.BlockSpec((6, None, radii, NL), lambda s: (0, s, 0, 0))
    sums = pl.pallas_call(
        functools.partial(synthesis_kernel, groups, width),
        grid=(slots,),
        in_specs=[
            pl.BlockSpec(memory_space=pltpu.SMEM),
            field_spec,
            field_spec,
            pl.BlockSpec((1, NLAT, NL), lambda s: (s, 0, 0)),
        ],
        out_specs=pl.BlockSpec((members * slots, 12 * width), lambda s: (0, 0)),
        out_shape=jax.ShapeDtypeStruct((members * slots, 12 * width), bf16),
        scratch_shapes=[
            pltpu.VMEM((12 * radii, NLAT), f32),
            pltpu.VMEM((groups, radii, 12 * width), f32),
            pltpu.VMEM((12 * width // LANES, members * slots, LANES), f32),
        ],
        name="synthesis",
    )(own_orders, velocity_rows, vorticity_rows, legendre_rows)
    pieces = lax.all_to_all(
        sums.reshape(members, slots, 12 * width), "ma", split_axis=0, concat_axis=0, tiled=True
    ).reshape(members * slots, 12 * width)

    coarse_cos, coarse_sin = angle_parts(order_table, LANES * jnp.arange(LANES, dtype=jnp.int32) % NLON)
    fine_cos, fine_sin = angle_parts(order_table, jnp.arange(LANES, dtype=jnp.int32))
    table = pl.pallas_call(
        harmonics_kernel,
        in_specs=[vmem] * 4,
        out_specs=vmem,
        out_shape=jax.ShapeDtypeStruct((2, NL, NLON), bf16),
        cost_estimate=pl.CostEstimate(flops=6 * NL * NLON, bytes_accessed=8 * NL * NLON, transcendentals=0),
        name="harmonics",
    )(coarse_cos, coarse_sin, fine_cos, fine_sin)

    tendency = pl.pallas_call(
        functools.partial(longitude_kernel, width),
        in_specs=[vmem] * 2,
        out_specs=vmem,
        out_shape=jax.ShapeDtypeStruct((NL, 6 * width), bf16),
        scratch_shapes=[pltpu.VMEM((NL, 6 * width), f32)],
        name="longitude",
    )(pieces, table)
    pieces = lax.all_to_all(
        tendency.reshape(members, slots, 6 * width), "ma", split_axis=0, concat_axis=0, tiled=True
    ).reshape(members * slots, 6 * width)

    lanes = 6 * slots * degrees
    tiles = pl.cdiv(6 * width, LANES)
    sides = pl.pallas_call(
        functools.partial(analysis_kernel, groups, width, degrees),
        in_specs=[vmem] * 3,
        out_specs=vmem,
        out_shape=jax.ShapeDtypeStruct((owners * radii, lanes), bf16),
        scratch_shapes=[
            pltpu.VMEM((tiles, members * slots, LANES), f32),
            pltpu.VMEM((slots, groups, radii, tiles * LANES), f32),
            pltpu.VMEM((slots, 6 * radii, NLAT), f32),
            pltpu.VMEM((slots, 6 * radii, NL), f32),
            pltpu.VMEM((owners * radii, lanes), f32),
        ],
        name="analysis",
    )(pieces, velocity_rows, weighted_rows)
    columns = lax.all_to_all(
        sides.reshape(owners, radii, lanes), "row", split_axis=0, concat_axis=0, tiled=True
    ).reshape(NR, lanes)

    advanced = pl.pallas_call(
        solve_kernel,
        in_specs=[vmem] * 2,
        out_specs=vmem,
        out_shape=jax.ShapeDtypeStruct((lanes, NR), f32),
        scratch_shapes=[pltpu.VMEM((lanes, NR), f32)],
        name="solve",
    )(columns, inverse_operators)
    return advanced.reshape(3, 2, slots, degrees, NR)


def solution(mesh):
    in_specs = (
        P(None, None, "ma", "row", None),
        P(None, None, "ma", "row", None),
        P(),
        P("ma", None, None),
        P("ma", None, None),
        P("row", None, None),
    )
    out_specs = P(None, None, "ma", "row", None)
    return jax.shard_map(
        per_device, mesh=mesh, in_specs=in_specs, out_specs=out_specs, check_vma=False
    )
```

```python
import functools
import math

import jax
import jax.numpy as jnp
from jax import lax
from jax.experimental import pallas as pl
from jax.experimental.pallas import tpu as pltpu
from jax.sharding import PartitionSpec as P

NL = 384
NLAT = 576
NLON = 1152
NR = 128
LANES = 128


time_step = 0.5
rotation = 2.0

NT_DIMS = (((1,), (1,)), ((), ()))


def dot(left, right, dims=(((1,), (0,)), ((), ()))):
    return lax.dot_general(left, right, dims, preferred_element_type=jnp.float32)


def angle_parts(orders, steps):
    phases = orders[:, None] * steps[None, :] % NLON
    angles = phases.astype(jnp.float32) * (2.0 * math.pi / NLON)
    return jnp.cos(angles), jnp.sin(angles)


def harmonics_kernel(coarse_cos, coarse_sin, fine_cos, fine_sin, table):
    cos_b = fine_cos[...]
    sin_b = fine_sin[...]
    for block in range(NLON // LANES):
        cos_a = coarse_cos[:, block : block + 1]
        sin_a = coarse_sin[:, block : block + 1]
        lanes = pl.ds(block * LANES, LANES)
        table[0, :, lanes] = (cos_a * cos_b - sin_a * sin_b).astype(jnp.bfloat16)
        table[1, :, lanes] = (-(sin_a * cos_b + cos_a * sin_b)).astype(jnp.bfloat16)


def lane_index():
    return lax.broadcasted_iota(jnp.int32, (8, LANES), 1)


def joined(pieces, width, tile):
    start = tile * LANES
    lanes = lane_index()
    result = None
    for index in range(start // width, min(len(pieces), (start + LANES - 1) // width + 1)):
        offset = index * width - start
        moved = pieces[index]
        if offset % LANES:
            moved = pltpu.roll(moved, offset % LANES, 1)
        result = moved if result is None else jnp.where(lanes >= offset, moved, result)
    return result


def parted(tiles, width, index):
    tile, offset = divmod(index * width, LANES)
    piece = tiles[tile]
    if offset + width > LANES:
        piece = jnp.where(lane_index() >= offset, piece, tiles[tile + 1])
    if offset:
        piece = pltpu.roll(piece, LANES - offset, 1)
    return piece


def synthesis_kernel(groups, width, orders, velocity, vorticity, legendre, out, stage):
    slot = pl.program_id(0)
    slots = orders.shape[0]
    radii = velocity.shape[1]
    count = 12 * radii
    own = jnp.where(orders[slot] == 0, 1.0, 2.0).astype(jnp.float32) / NL
    spectral = jnp.concatenate([velocity[...], vorticity[...]], axis=0)
    spectral = spectral.astype(jnp.float32).reshape(count, NL).astype(jnp.bfloat16)
    rows = pl.ds(pl.multiple_of(slot * count, 8), count)
    for group in range(groups):
        part = dot(spectral, legendre[0, group * width : (group + 1) * width, :], NT_DIMS)
        stage[group, rows, :width] = part * own

    @pl.when(slot == slots - 1)
    def finish():
        def receiver(index, carry):
            group, radius = index // radii, index % radii
            pieces = [
                stage[group, pl.ds((component * 2 + part) * radii + radius, slots, stride=count), :]
                for part in range(2)
                for component in range(6)
            ]
            target = pl.ds(pl.multiple_of(index * slots, 8), slots)
            for tile in range(12 * width // LANES):
                lanes = slice(tile * LANES, (tile + 1) * LANES)
                out[target, lanes] = joined(pieces, width, tile).astype(jnp.bfloat16)
            return carry

        lax.fori_loop(0, groups * radii, receiver, 0, unroll=4)


def longitude_kernel(width, received, table, out, stage):
    points = 6 * width
    turned = received[...].astype(jnp.float32).T.astype(jnp.bfloat16)
    grid = dot(turned[:points], table[0]) + dot(turned[points:], table[1])
    u = [grid[c * width : (c + 1) * width] for c in range(3)]
    w = [grid[(3 + c) * width : (4 + c) * width] for c in range(3)]
    spin = w[2] + rotation
    products = jnp.concatenate(
        [
            u[1] * spin - u[2] * w[1],
            u[2] * w[0] - u[0] * spin,
            u[0] * w[1] - u[1] * w[0],
        ],
        axis=0,
    ).astype(jnp.bfloat16)
    for part in range(2):
        back = dot(table[part], products, NT_DIMS) * (NL / NLON)
        stage[:, part * 3 * width : (part + 1) * 3 * width] = back
    out[...] = stage[...].astype(jnp.bfloat16)


def analysis_kernel(groups, width, received, velocity, weighted, out, whole, side):
    slots = weighted.shape[0]
    radii = velocity.shape[2]
    tiles = whole.shape[0]
    for tile in range(tiles):
        size = min(LANES, 6 * width - tile * LANES)
        whole[tile, :, :size] = received[:, tile * LANES : tile * LANES + size].astype(jnp.float32)
    for slot in range(slots):
        terms = None
        for group in range(groups):
            source = pl.ds(group * radii * slots + slot, radii, stride=slots)
            parts = [whole[tile, source, :] for tile in range(tiles)]
            fields = [parted(parts, width, part * 3 + component) for component in range(3) for part in range(2)]
            block = jnp.concatenate(fields, axis=0)[:, :width].astype(jnp.bfloat16)
            term = dot(block, weighted[slot, group * width : (group + 1) * width, :])
            terms = term if terms is None else terms + term
        known = velocity[:, slot].astype(jnp.float32).reshape(6 * radii, NL)
        right_side = known + time_step * terms
        for field in range(6):
            for tile in range(NL // LANES):
                side[tile, pl.ds(field * slots + slot, radii, stride=6 * slots), :] = right_side[
                    field * radii : (field + 1) * radii, tile * LANES : (tile + 1) * LANES
                ]
    for tile in range(NL // LANES):
        out[tile * LANES : (tile + 1) * LANES, :] = side[tile].T.astype(jnp.bfloat16)


def solve_kernel(received, operators, out, whole, square):
    degrees = operators.shape[0]
    owners = received.shape[0] // degrees
    radii = NR // owners
    count = received.shape[1] // radii
    tiles = whole.shape[0]
    for tile in range(tiles):
        whole[tile] = received[:, tile * LANES : (tile + 1) * LANES].astype(jnp.float32)

    def solve(degree, carry):
        for half in range(owners // 8):
            source = pl.ds(half * 8 * degrees + degree, 8, stride=degrees)
            parts = [whole[tile, source, :] for tile in range(tiles)]
            for radius in range(radii):
                target = pl.ds(half * 8 * radii + radius, 8, stride=radii)
                square[degree, target, :] = parted(parts, count, radius)
        columns = square[degree].T[:count].astype(jnp.bfloat16)
        operator = operators[degree]
        high = operator.astype(jnp.bfloat16)
        low = (operator - high.astype(jnp.float32)).astype(jnp.bfloat16)
        out[pl.ds(degree, count, stride=degrees), :] = dot(columns, high, NT_DIMS) + dot(columns, low, NT_DIMS)
        return carry

    lax.fori_loop(0, degrees, solve, 0, unroll=4)


def per_device(velocity, vorticity, order_table, legendre_bf, weighted, inverse_operators):
    slots = velocity.shape[2]
    radii = velocity.shape[3]
    degrees = inverse_operators.shape[0]
    members = NL // slots
    owners = NL // degrees
    groups = members // radii
    width = NLAT // groups
    f32, bf16 = jnp.float32, jnp.bfloat16
    vmem = pl.BlockSpec(memory_space=pltpu.VMEM)
    params = pltpu.CompilerParams(vmem_limit_bytes=24 * 2**20)

    own_orders = lax.dynamic_slice_in_dim(order_table, lax.axis_index("ma") * slots, slots)
    velocity_rows = velocity.reshape(6, slots, radii, NL)
    vorticity_rows = vorticity.reshape(6, slots, radii, NL)
    legendre_rows = jnp.swapaxes(legendre_bf, 1, 2)
    weighted_rows = jnp.swapaxes(weighted, 1, 2)

    field_spec = pl.BlockSpec((6, None, radii, NL), lambda s: (0, s, 0, 0))
    sums = pl.pallas_call(
        functools.partial(synthesis_kernel, groups, width),
        grid=(slots,),
        in_specs=[
            pl.BlockSpec(memory_space=pltpu.SMEM),
            field_spec,
            field_spec,
            pl.BlockSpec((1, NLAT, NL), lambda s: (s, 0, 0)),
        ],
        out_specs=pl.BlockSpec((members * slots, 12 * width), lambda s: (0, 0)),
        out_shape=jax.ShapeDtypeStruct((members * slots, 12 * width), bf16),
        scratch_shapes=[
            pltpu.VMEM((groups, slots * 12 * radii, LANES), f32),
        ],
        name="synthesis",
    )(own_orders, velocity_rows, vorticity_rows, legendre_rows)
    pieces = lax.all_to_all(
        sums.reshape(members, slots, 12 * width), "ma", split_axis=0, concat_axis=0, tiled=True
    ).reshape(members * slots, 12 * width)

    coarse_cos, coarse_sin = angle_parts(order_table, LANES * jnp.arange(LANES, dtype=jnp.int32) % NLON)
    fine_cos, fine_sin = angle_parts(order_table, jnp.arange(LANES, dtype=jnp.int32))
    table = pl.pallas_call(
        harmonics_kernel,
        in_specs=[vmem] * 4,
        out_specs=vmem,
        out_shape=jax.ShapeDtypeStruct((2, NL, NLON), bf16),
        cost_estimate=pl.CostEstimate(flops=6 * NL * NLON, bytes_accessed=8 * NL * NLON, transcendentals=0),
        compiler_params=params,
        name="harmonics",
    )(coarse_cos, coarse_sin, fine_cos, fine_sin)

    tendency = pl.pallas_call(
        functools.partial(longitude_kernel, width),
        in_specs=[vmem] * 2,
        out_specs=vmem,
        out_shape=jax.ShapeDtypeStruct((NL, 6 * width), bf16),
        scratch_shapes=[pltpu.VMEM((NL, 6 * width), f32)],
        compiler_params=params,
        name="longitude",
    )(pieces, table)
    pieces = lax.all_to_all(
        tendency.reshape(members, slots, 6 * width), "ma", split_axis=0, concat_axis=0, tiled=True
    ).reshape(members * slots, 6 * width)

    lanes = 6 * slots * radii
    sides = pl.pallas_call(
        functools.partial(analysis_kernel, groups, width),
        in_specs=[vmem] * 3,
        out_specs=vmem,
        out_shape=jax.ShapeDtypeStruct((NL, lanes), bf16),
        scratch_shapes=[
            pltpu.VMEM((pl.cdiv(6 * width, LANES), members * slots, LANES), f32),
            pltpu.VMEM((NL // LANES, lanes, LANES), f32),
        ],
        compiler_params=params,
        name="analysis",
    )(pieces, velocity_rows, weighted_rows)
    columns = lax.all_to_all(
        sides.reshape(owners, degrees, lanes), "row", split_axis=0, concat_axis=0, tiled=True
    ).reshape(NL, lanes)

    advanced = pl.pallas_call(
        solve_kernel,
        in_specs=[vmem] * 2,
        out_specs=vmem,
        out_shape=jax.ShapeDtypeStruct((6 * slots * degrees, NR), f32),
        scratch_shapes=[
            pltpu.VMEM((lanes // LANES, NL, LANES), f32),
            pltpu.VMEM((degrees, NR, LANES), f32),
        ],
        compiler_params=params,
        name="solve",
    )(columns, inverse_operators)
    return advanced.reshape(3, 2, slots, degrees, NR)


def solution(mesh):
    in_specs = (
        P(None, None, "ma", "row", None),
        P(None, None, "ma", "row", None),
        P(),
        P("ma", None, None),
        P("ma", None, None),
        P("row", None, None),
    )
    out_specs = P(None, None, "ma", "row", None)
    return jax.shard_map(
        per_device, mesh=mesh, in_specs=in_specs, out_specs=out_specs, check_vma=False
    )
```

```python
import functools
import math

import jax
import jax.numpy as jnp
from jax import lax
from jax.experimental import pallas as pl
from jax.experimental.pallas import tpu as pltpu
from jax.sharding import PartitionSpec as P

NL = 384
NLAT = 576
NLON = 1152
NR = 128
LANES = 128


time_step = 0.5
rotation = 2.0

NT_DIMS = (((1,), (1,)), ((), ()))


def dot(left, right, dims=(((1,), (0,)), ((), ()))):
    return lax.dot_general(left, right, dims, preferred_element_type=jnp.float32)


def angle_parts(orders, steps):
    phases = orders[:, None] * steps[None, :] % NLON
    angles = phases.astype(jnp.float32) * (2.0 * math.pi / NLON)
    return jnp.cos(angles), jnp.sin(angles)


def harmonics_kernel(coarse_cos, coarse_sin, fine_cos, fine_sin, table):
    cos_b = fine_cos[...]
    sin_b = fine_sin[...]
    for block in range(NLON // LANES):
        cos_a = coarse_cos[:, block : block + 1]
        sin_a = coarse_sin[:, block : block + 1]
        lanes = pl.ds(block * LANES, LANES)
        table[:NL, lanes] = (cos_a * cos_b - sin_a * sin_b).astype(jnp.bfloat16)
        table[NL:, lanes] = (-(sin_a * cos_b + cos_a * sin_b)).astype(jnp.bfloat16)


def lane_index():
    return lax.broadcasted_iota(jnp.int32, (8, LANES), 1)


def joined(pieces, width, tile):
    start = tile * LANES
    lanes = lane_index()
    result = None
    for index in range(start // width, min(len(pieces), (start + LANES - 1) // width + 1)):
        offset = index * width - start
        moved = pieces[index]
        if offset % LANES:
            moved = pltpu.roll(moved, offset % LANES, 1)
        result = moved if result is None else jnp.where(lanes >= offset, moved, result)
    return result


def parted(tiles, width, index):
    tile, offset = divmod(index * width, LANES)
    piece = tiles[tile]
    if offset + width > LANES:
        piece = jnp.where(lane_index() >= offset, piece, tiles[tile + 1])
    if offset:
        piece = pltpu.roll(piece, LANES - offset, 1)
    return piece


def synthesis_kernel(
    groups, width, orders, velocity, vorticity, legendre, out, fields, tables, stage, turned, field_sems, table_sems
):
    slots = tables.shape[0]
    radii = fields.shape[3]
    copies = [
        pltpu.make_async_copy(source, fields.at[index], field_sems.at[index])
        for index, source in enumerate((velocity, vorticity))
    ]
    loads = [
        pltpu.make_async_copy(legendre.at[slot], tables.at[slot], table_sems.at[slot]) for slot in range(slots)
    ]
    for copy in copies + loads:
        copy.start()
    for copy in copies:
        copy.wait()
    first = lax.axis_index("ma") * slots
    for slot in range(slots):
        own = jnp.where(orders[first + slot] == 0, 1.0, 2.0).astype(jnp.float32) / NL
        spectral = fields[:, :, slot].astype(jnp.float32).reshape(12 * radii, NL).astype(jnp.bfloat16)
        loads[slot].wait()
        for group in range(groups):
            part = dot(spectral, tables[slot, group * width : (group + 1) * width, :], NT_DIMS) * own
            for field in range(12):
                stage[field, slot * radii : (slot + 1) * radii, group * LANES : group * LANES + width] = part[
                    field * radii : (field + 1) * radii
                ]
    count = slots * radii
    row = lax.broadcasted_iota(jnp.int32, (count, count), 0)
    column = lax.broadcasted_iota(jnp.int32, (count, count), 1)
    swap = (column == row % slots * radii + row // slots).astype(jnp.float32).astype(jnp.bfloat16)
    for field in range(12):
        turned[field] = dot(swap, stage[field].astype(jnp.bfloat16))
    for group in range(groups):
        for radius in range(radii):
            pieces = [
                turned[component * 2 + part, radius * slots : (radius + 1) * slots, group * LANES : (group + 1) * LANES]
                for part in range(2)
                for component in range(6)
            ]
            target = (group * radii + radius) * slots
            for tile in range(12 * width // LANES):
                out[target : target + slots, tile * LANES : (tile + 1) * LANES] = joined(pieces, width, tile).astype(
                    jnp.bfloat16
                )


def longitude_kernel(width, received, table, out, stage):
    points = 6 * width
    turned = received[...].astype(jnp.float32).T.astype(jnp.bfloat16)
    grid = dot(jnp.concatenate([turned[:points], turned[points:]], axis=1), table[...])
    u = [grid[c * width : (c + 1) * width] for c in range(3)]
    w = [grid[(3 + c) * width : (4 + c) * width] for c in range(3)]
    spin = w[2] + rotation
    products = jnp.concatenate(
        [
            u[1] * spin - u[2] * w[1],
            u[2] * w[0] - u[0] * spin,
            u[0] * w[1] - u[1] * w[0],
        ],
        axis=0,
    ).astype(jnp.bfloat16)
    back = (dot(products, table[...], NT_DIMS) * (NL / NLON)).T
    for part in range(2):
        stage[:, part * 3 * width : (part + 1) * 3 * width] = back[part * NL : (part + 1) * NL]
    out[...] = stage[...].astype(jnp.bfloat16)


def analysis_kernel(groups, width, received, velocity, weighted, out, whole, side):
    slots = weighted.shape[0]
    radii = velocity.shape[2]
    tiles = whole.shape[0]
    for tile in range(tiles):
        size = min(LANES, 6 * width - tile * LANES)
        whole[tile, :, :size] = received[:, tile * LANES : tile * LANES + size].astype(jnp.float32)
    for slot in range(slots):
        terms = None
        for group in range(groups):
            source = pl.ds(group * radii * slots + slot, radii, stride=slots)
            parts = [whole[tile, source, :] for tile in range(tiles)]
            fields = [parted(parts, width, part * 3 + component) for component in range(3) for part in range(2)]
            block = jnp.concatenate(fields, axis=0)[:, :width].astype(jnp.bfloat16)
            term = dot(block, weighted[slot, group * width : (group + 1) * width, :])
            terms = term if terms is None else terms + term
        known = velocity[:, slot].astype(jnp.float32).reshape(6 * radii, NL)
        right_side = known + time_step * terms
        for field in range(6):
            for tile in range(NL // LANES):
                side[tile, pl.ds(field * slots + slot, radii, stride=6 * slots), :] = right_side[
                    field * radii : (field + 1) * radii, tile * LANES : (tile + 1) * LANES
                ]
    for tile in range(NL // LANES):
        out[tile * LANES : (tile + 1) * LANES, :] = side[tile].T.astype(jnp.bfloat16)


def operators_kernel(radii, operators, out):
    degrees = operators.shape[0]
    owners = NR // radii
    row = lax.broadcasted_iota(jnp.int32, (NR, NR), 0)
    column = lax.broadcasted_iota(jnp.int32, (NR, NR), 1)
    swap = (row == column % owners * radii + column // owners).astype(jnp.float32).astype(jnp.bfloat16)
    for degree in range(degrees):
        operator = operators[degree]
        high = operator.astype(jnp.bfloat16)
        low = (operator - high.astype(jnp.float32)).astype(jnp.bfloat16)
        out[degree, :, :NR] = dot(high, swap).astype(jnp.bfloat16)
        out[degree, :, NR:] = dot(low, swap).astype(jnp.bfloat16)


def solve_kernel(radii, received, operators, out, whole, results):
    degrees = operators.shape[0]
    owners = NR // radii
    count = received.shape[1] // radii
    tiles = whole.shape[0]
    for tile in range(tiles):
        whole[tile] = received[:, tile * LANES : (tile + 1) * LANES].astype(jnp.float32)
    for degree in range(degrees):
        halves = [
            [whole[tile, pl.ds(half * 8 * degrees + degree, 8, stride=degrees), :] for tile in range(tiles)]
            for half in range(owners // 8)
        ]
        pieces = [parted(parts, count, radius) for radius in range(radii) for parts in halves]
        columns = jnp.concatenate(pieces, axis=0).T[:count].astype(jnp.bfloat16)
        both = jnp.concatenate([columns, columns], axis=1)
        results[degree * count : (degree + 1) * count, :] = dot(both, operators[degree], NT_DIMS)
    for row in range(count):
        out[row * degrees : (row + 1) * degrees, :] = results[pl.ds(row, degrees, stride=count), :]


def per_device(velocity, vorticity, order_table, legendre_bf, weighted, inverse_operators):
    slots = velocity.shape[2]
    radii = velocity.shape[3]
    degrees = inverse_operators.shape[0]
    members = NL // slots
    owners = NL // degrees
    groups = members // radii
    width = NLAT // groups
    f32, bf16 = jnp.float32, jnp.bfloat16
    vmem = pl.BlockSpec(memory_space=pltpu.VMEM)
    params = pltpu.CompilerParams(vmem_limit_bytes=24 * 2**20)

    velocity_rows = velocity.reshape(6, slots, radii, NL)
    vorticity_rows = vorticity.reshape(6, slots, radii, NL)
    legendre_rows = jnp.swapaxes(legendre_bf, 1, 2)
    weighted_rows = jnp.swapaxes(weighted, 1, 2)

    hbm = pl.BlockSpec(memory_space=pl.ANY)
    sums = pl.pallas_call(
        functools.partial(synthesis_kernel, groups, width),
        in_specs=[pl.BlockSpec(memory_space=pltpu.SMEM), hbm, hbm, hbm],
        out_specs=vmem,
        out_shape=jax.ShapeDtypeStruct((members * slots, 12 * width), bf16),
        scratch_shapes=[
            pltpu.VMEM((2, 6, slots, radii, NL), bf16),
            pltpu.VMEM((slots, NLAT, NL), bf16),
            pltpu.VMEM((12, slots * radii, groups * LANES), f32),
            pltpu.VMEM((12, slots * radii, groups * LANES), f32),
            pltpu.SemaphoreType.DMA((2,)),
            pltpu.SemaphoreType.DMA((slots,)),
        ],
        compiler_params=pltpu.CompilerParams(vmem_limit_bytes=60 * 2**20),
        name="synthesis",
    )(order_table, velocity_rows, vorticity_rows, legendre_rows)
    pieces = lax.all_to_all(
        sums.reshape(members, slots, 12 * width), "ma", split_axis=0, concat_axis=0, tiled=True
    ).reshape(members * slots, 12 * width)

    coarse_cos, coarse_sin = angle_parts(order_table, LANES * jnp.arange(LANES, dtype=jnp.int32) % NLON)
    fine_cos, fine_sin = angle_parts(order_table, jnp.arange(LANES, dtype=jnp.int32))
    table = pl.pallas_call(
        harmonics_kernel,
        in_specs=[vmem] * 4,
        out_specs=vmem,
        out_shape=jax.ShapeDtypeStruct((2 * NL, NLON), bf16),
        cost_estimate=pl.CostEstimate(flops=6 * NL * NLON, bytes_accessed=8 * NL * NLON, transcendentals=0),
        compiler_params=params,
        name="harmonics",
    )(coarse_cos, coarse_sin, fine_cos, fine_sin)

    operators = pl.pallas_call(
        functools.partial(operators_kernel, radii),
        in_specs=[vmem],
        out_specs=vmem,
        out_shape=jax.ShapeDtypeStruct((degrees, NR, 2 * NR), bf16),
        cost_estimate=pl.CostEstimate(
            flops=4 * degrees * NR**3, bytes_accessed=8 * degrees * NR * NR, transcendentals=0
        ),
        compiler_params=params,
        name="operators",
    )(inverse_operators)

    tendency = pl.pallas_call(
        functools.partial(longitude_kernel, width),
        in_specs=[vmem] * 2,
        out_specs=vmem,
        out_shape=jax.ShapeDtypeStruct((NL, 6 * width), bf16),
        scratch_shapes=[pltpu.VMEM((NL, 6 * width), f32)],
        compiler_params=params,
        name="longitude",
    )(pieces, table)
    pieces = lax.all_to_all(
        tendency.reshape(members, slots, 6 * width), "ma", split_axis=0, concat_axis=0, tiled=True
    ).reshape(members * slots, 6 * width)

    lanes = 6 * slots * radii
    sides = pl.pallas_call(
        functools.partial(analysis_kernel, groups, width),
        in_specs=[vmem] * 3,
        out_specs=vmem,
        out_shape=jax.ShapeDtypeStruct((NL, lanes), bf16),
        scratch_shapes=[
            pltpu.VMEM((pl.cdiv(6 * width, LANES), members * slots, LANES), f32),
            pltpu.VMEM((NL // LANES, lanes, LANES), f32),
        ],
        compiler_params=params,
        name="analysis",
    )(pieces, velocity_rows, weighted_rows)
    columns = lax.all_to_all(
        sides.reshape(owners, degrees, lanes), "row", split_axis=0, concat_axis=0, tiled=True
    ).reshape(NL, lanes)

    advanced = pl.pallas_call(
        functools.partial(solve_kernel, radii),
        in_specs=[vmem] * 2,
        out_specs=vmem,
        out_shape=jax.ShapeDtypeStruct((6 * slots * degrees, NR), f32),
        scratch_shapes=[
            pltpu.VMEM((lanes // LANES, NL, LANES), f32),
            pltpu.VMEM((6 * slots * degrees, NR), f32),
        ],
        compiler_params=params,
        name="solve",
    )(columns, operators)
    return advanced.reshape(3, 2, slots, degrees, NR)


def solution(mesh):
    in_specs = (
        P(None, None, "ma", "row", None),
        P(None, None, "ma", "row", None),
        P(),
        P("ma", None, None),
        P("ma", None, None),
        P("row", None, None),
    )
    out_specs = P(None, None, "ma", "row", None)
    return jax.shard_map(
        per_device, mesh=mesh, in_specs=in_specs, out_specs=out_specs, check_vma=False
    )
```

```python
import functools
import math

import jax
import jax.numpy as jnp
from jax import lax
from jax.experimental import pallas as pl
from jax.experimental.pallas import tpu as pltpu
from jax.sharding import PartitionSpec as P

NL = 384
NLAT = 576
NLON = 1152
NR = 128
LANES = 128


time_step = 0.5
rotation = 2.0

NT_DIMS = (((1,), (1,)), ((), ()))


def dot(left, right, dims=(((1,), (0,)), ((), ()))):
    return lax.dot_general(left, right, dims, preferred_element_type=jnp.float32)


def angle_parts(orders, steps):
    phases = orders[:, None] * steps[None, :] % NLON
    angles = phases.astype(jnp.float32) * (2.0 * math.pi / NLON)
    return jnp.cos(angles), jnp.sin(angles)


def harmonics_kernel(coarse_cos, coarse_sin, fine_cos, fine_sin, table):
    cos_b = fine_cos[...]
    sin_b = fine_sin[...]
    for block in range(NLON // LANES):
        cos_a = coarse_cos[:, block : block + 1]
        sin_a = coarse_sin[:, block : block + 1]
        lanes = pl.ds(block * LANES, LANES)
        table[:NL, lanes] = (cos_a * cos_b - sin_a * sin_b).astype(jnp.bfloat16)
        table[NL:, lanes] = (-(sin_a * cos_b + cos_a * sin_b)).astype(jnp.bfloat16)


def lane_index():
    return lax.broadcasted_iota(jnp.int32, (8, LANES), 1)


def joined(pieces, width, tile):
    start = tile * LANES
    lanes = lane_index()
    result = None
    for index in range(start // width, min(len(pieces), (start + LANES - 1) // width + 1)):
        offset = index * width - start
        moved = pieces[index]
        if offset % LANES:
            moved = pltpu.roll(moved, offset % LANES, 1)
        result = moved if result is None else jnp.where(lanes >= offset, moved, result)
    return result


def parted(tiles, width, index):
    tile, offset = divmod(index * width, LANES)
    piece = tiles[tile]
    if offset + width > LANES:
        piece = jnp.where(lane_index() >= offset, piece, tiles[tile + 1])
    if offset:
        piece = pltpu.roll(piece, LANES - offset, 1)
    return piece


def synthesis_kernel(
    groups,
    width,
    order_table,
    velocity,
    vorticity,
    legendre,
    out,
    orders,
    fields,
    tables,
    stage,
    turned,
    blocks,
    order_sem,
    field_sems,
    table_sems,
    block_sems,
):
    slots = tables.shape[0]
    radii = fields.shape[3]
    copies = [
        pltpu.make_async_copy(source, fields.at[index], field_sems.at[index])
        for index, source in enumerate((velocity, vorticity))
    ]
    loads = [
        pltpu.make_async_copy(legendre.at[slot, pl.ds(0, NLAT // 2)], tables.at[slot], table_sems.at[slot])
        for slot in range(slots)
    ]
    copies.append(pltpu.make_async_copy(order_table, orders, order_sem))
    for copy in copies + loads:
        copy.start()
    for copy in copies + loads:
        copy.wait()
    first = lax.axis_index("ma") * slots
    count = 12 * radii
    even = lax.broadcasted_iota(jnp.int32, (count, NL), 1) % 2 == 0
    for slot in range(slots):
        order = orders[first + slot]
        own = jnp.where(order == 0, 1.0, 2.0).astype(jnp.float32) / NL
        mirrored = jnp.where(order % 2 == 0, own, -own)
        spectral = fields[:, :, slot].astype(jnp.float32).reshape(count, NL)
        low = jnp.where(even, spectral, 0.0)
        both = jnp.concatenate([low, spectral - low], axis=0).astype(jnp.bfloat16)
        for group in range(groups // 2):
            sums = dot(both, tables[slot, group * width : (group + 1) * width, :], NT_DIMS)
            for hemisphere, part in enumerate(
                ((sums[:count] + sums[count:]) * own, (sums[:count] - sums[count:]) * mirrored)
            ):
                lane = (group + hemisphere * groups // 2) * LANES
                for field in range(12):
                    stage[field, slot * radii : (slot + 1) * radii, lane : lane + width] = part[
                        field * radii : (field + 1) * radii
                    ]
    count = slots * radii
    row = lax.broadcasted_iota(jnp.int32, (count, count), 0)
    column = lax.broadcasted_iota(jnp.int32, (count, count), 1)
    swap = (column == row % slots * radii + row // slots).astype(jnp.float32).astype(jnp.bfloat16)
    for field in range(12):
        turned[field] = dot(swap, stage[field].astype(jnp.bfloat16))
    stores = []
    for group in range(groups):
        for radius in range(radii):
            pieces = [
                turned[component * 2 + part, radius * slots : (radius + 1) * slots, group * LANES : (group + 1) * LANES]
                for part in range(2)
                for component in range(6)
            ]
            target = (group * radii + radius) * slots
            for tile in range(12 * width // LANES):
                blocks[target : target + slots, tile * LANES : (tile + 1) * LANES] = joined(
                    pieces, width, tile
                ).astype(jnp.bfloat16)
        rows = pl.ds(group * radii * slots, radii * slots)
        stores.append(pltpu.make_async_copy(blocks.at[rows], out.at[rows], block_sems.at[group]))
        stores[-1].start()
    for copy in stores:
        copy.wait()


def longitude_kernel(width, received, table, out, stage):
    points = 6 * width
    turned = received[...].astype(jnp.float32).T.astype(jnp.bfloat16)
    grid = dot(jnp.concatenate([turned[:points], turned[points:]], axis=1), table[...])
    u = [grid[c * width : (c + 1) * width] for c in range(3)]
    w = [grid[(3 + c) * width : (4 + c) * width] for c in range(3)]
    spin = w[2] + rotation
    products = jnp.concatenate(
        [
            u[1] * spin - u[2] * w[1],
            u[2] * w[0] - u[0] * spin,
            u[0] * w[1] - u[1] * w[0],
        ],
        axis=0,
    ).astype(jnp.bfloat16)
    back = (dot(products, table[...], NT_DIMS) * (NL / NLON)).T
    for part in range(2):
        stage[:, part * 3 * width : (part + 1) * 3 * width] = back[part * NL : (part + 1) * NL]
    out[...] = stage[...].astype(jnp.bfloat16)


def analysis_kernel(groups, width, orders, received, velocity, weighted, out, whole, side):
    slots = weighted.shape[0]
    radii = velocity.shape[2]
    tiles = whole.shape[0]
    for tile in range(tiles):
        size = min(LANES, 6 * width - tile * LANES)
        whole[tile, :, :size] = received[:, tile * LANES : tile * LANES + size].astype(jnp.float32)
    first = lax.axis_index("ma") * slots
    count = 6 * radii
    degree = lax.broadcasted_iota(jnp.int32, (count, NL), 1)
    for slot in range(slots):
        total = None
        for group in range(groups // 2):
            fields = []
            for block in (group, group + groups // 2):
                source = pl.ds(block * radii * slots + slot, radii, stride=slots)
                parts = [whole[tile, source, :] for tile in range(tiles)]
                fields += [parted(parts, width, part * 3 + component) for component in range(3) for part in range(2)]
            both = jnp.concatenate(fields, axis=0)[:, :width].astype(jnp.bfloat16)
            term = dot(both, weighted[slot, group * width : (group + 1) * width, :])
            total = term if total is None else total + term
        odd = (degree + orders[first + slot]) % 2 == 1
        terms = total[:count] + jnp.where(odd, -total[count:], total[count:])
        known = velocity[:, slot].astype(jnp.float32).reshape(6 * radii, NL)
        right_side = known + time_step * terms
        for field in range(6):
            for tile in range(NL // LANES):
                side[tile, pl.ds(field * slots + slot, radii, stride=6 * slots), :] = right_side[
                    field * radii : (field + 1) * radii, tile * LANES : (tile + 1) * LANES
                ]
    for tile in range(NL // LANES):
        out[tile * LANES : (tile + 1) * LANES, :] = side[tile].T.astype(jnp.bfloat16)


def operators_kernel(radii, operators, out):
    degrees = operators.shape[0]
    owners = NR // radii
    row = lax.broadcasted_iota(jnp.int32, (NR, NR), 0)
    column = lax.broadcasted_iota(jnp.int32, (NR, NR), 1)
    swap = (row == column % owners * radii + column // owners).astype(jnp.float32).astype(jnp.bfloat16)
    for degree in range(degrees):
        operator = operators[degree]
        high = operator.astype(jnp.bfloat16)
        low = (operator - high.astype(jnp.float32)).astype(jnp.bfloat16)
        out[degree, :, :NR] = dot(high, swap).astype(jnp.bfloat16)
        out[degree, :, NR:] = dot(low, swap).astype(jnp.bfloat16)


def solve_kernel(radii, received, operators, out, whole, results):
    degrees = operators.shape[0]
    owners = NR // radii
    count = received.shape[1] // radii
    tiles = whole.shape[0]
    for tile in range(tiles):
        whole[tile] = received[:, tile * LANES : (tile + 1) * LANES].astype(jnp.float32)
    for degree in range(degrees):
        halves = [
            [whole[tile, pl.ds(half * 8 * degrees + degree, 8, stride=degrees), :] for tile in range(tiles)]
            for half in range(owners // 8)
        ]
        pieces = [parted(parts, count, radius) for radius in range(radii) for parts in halves]
        columns = jnp.concatenate(pieces, axis=0).T[:count].astype(jnp.bfloat16)
        both = jnp.concatenate([columns, columns], axis=1)
        results[degree * count : (degree + 1) * count, :] = dot(both, operators[degree], NT_DIMS)
    for row in range(count):
        out[row * degrees : (row + 1) * degrees, :] = results[pl.ds(row, degrees, stride=count), :]


def per_device(velocity, vorticity, order_table, legendre_bf, weighted, inverse_operators):
    slots = velocity.shape[2]
    radii = velocity.shape[3]
    degrees = inverse_operators.shape[0]
    members = NL // slots
    owners = NL // degrees
    groups = members // radii
    width = NLAT // groups
    f32, bf16 = jnp.float32, jnp.bfloat16
    vmem = pl.BlockSpec(memory_space=pltpu.VMEM)
    params = pltpu.CompilerParams(vmem_limit_bytes=24 * 2**20)

    velocity_rows = velocity.reshape(6, slots, radii, NL)
    vorticity_rows = vorticity.reshape(6, slots, radii, NL)
    legendre_rows = jnp.swapaxes(legendre_bf, 1, 2)
    weighted_rows = jnp.swapaxes(weighted, 1, 2)

    hbm = pl.BlockSpec(memory_space=pl.ANY)
    sums = pl.pallas_call(
        functools.partial(synthesis_kernel, groups, width),
        in_specs=[hbm] * 4,
        out_specs=hbm,
        out_shape=jax.ShapeDtypeStruct((members * slots, 12 * width), bf16),
        scratch_shapes=[
            pltpu.SMEM((NL,), jnp.int32),
            pltpu.VMEM((2, 6, slots, radii, NL), bf16),
            pltpu.VMEM((slots, NLAT // 2, NL), bf16),
            pltpu.VMEM((12, slots * radii, groups * LANES), f32),
            pltpu.VMEM((12, slots * radii, groups * LANES), f32),
            pltpu.VMEM((members * slots, 12 * width), bf16),
            pltpu.SemaphoreType.DMA,
            pltpu.SemaphoreType.DMA((2,)),
            pltpu.SemaphoreType.DMA((slots,)),
            pltpu.SemaphoreType.DMA((groups,)),
        ],
        compiler_params=pltpu.CompilerParams(vmem_limit_bytes=60 * 2**20),
        name="synthesis",
    )(order_table, velocity_rows, vorticity_rows, legendre_rows)
    pieces = lax.all_to_all(
        sums.reshape(members, slots, 12 * width), "ma", split_axis=0, concat_axis=0, tiled=True
    ).reshape(members * slots, 12 * width)

    coarse_cos, coarse_sin = angle_parts(order_table, LANES * jnp.arange(LANES, dtype=jnp.int32) % NLON)
    fine_cos, fine_sin = angle_parts(order_table, jnp.arange(LANES, dtype=jnp.int32))
    table = pl.pallas_call(
        harmonics_kernel,
        in_specs=[vmem] * 4,
        out_specs=vmem,
        out_shape=jax.ShapeDtypeStruct((2 * NL, NLON), bf16),
        cost_estimate=pl.CostEstimate(flops=6 * NL * NLON, bytes_accessed=8 * NL * NLON, transcendentals=0),
        compiler_params=params,
        name="harmonics",
    )(coarse_cos, coarse_sin, fine_cos, fine_sin)

    operators = pl.pallas_call(
        functools.partial(operators_kernel, radii),
        in_specs=[vmem],
        out_specs=vmem,
        out_shape=jax.ShapeDtypeStruct((degrees, NR, 2 * NR), bf16),
        cost_estimate=pl.CostEstimate(
            flops=4 * degrees * NR**3, bytes_accessed=8 * degrees * NR * NR, transcendentals=0
        ),
        compiler_params=params,
        name="operators",
    )(inverse_operators)
    table, operators = lax.optimization_barrier((table, operators))

    tendency = pl.pallas_call(
        functools.partial(longitude_kernel, width),
        in_specs=[vmem] * 2,
        out_specs=vmem,
        out_shape=jax.ShapeDtypeStruct((NL, 6 * width), bf16),
        scratch_shapes=[pltpu.VMEM((NL, 6 * width), f32)],
        compiler_params=params,
        name="longitude",
    )(pieces, table)
    pieces = lax.all_to_all(
        tendency.reshape(members, slots, 6 * width), "ma", split_axis=0, concat_axis=0, tiled=True
    ).reshape(members * slots, 6 * width)

    lanes = 6 * slots * radii
    sides = pl.pallas_call(
        functools.partial(analysis_kernel, groups, width),
        in_specs=[pl.BlockSpec(memory_space=pltpu.SMEM)] + [vmem] * 3,
        out_specs=vmem,
        out_shape=jax.ShapeDtypeStruct((NL, lanes), bf16),
        scratch_shapes=[
            pltpu.VMEM((pl.cdiv(6 * width, LANES), members * slots, LANES), f32),
            pltpu.VMEM((NL // LANES, lanes, LANES), f32),
        ],
        compiler_params=params,
        name="analysis",
    )(order_table, pieces, velocity_rows, weighted_rows)
    columns = lax.all_to_all(
        sides.reshape(owners, degrees, lanes), "row", split_axis=0, concat_axis=0, tiled=True
    ).reshape(NL, lanes)

    advanced = pl.pallas_call(
        functools.partial(solve_kernel, radii),
        in_specs=[vmem] * 2,
        out_specs=vmem,
        out_shape=jax.ShapeDtypeStruct((6 * slots * degrees, NR), f32),
        scratch_shapes=[
            pltpu.VMEM((lanes // LANES, NL, LANES), f32),
            pltpu.VMEM((6 * slots * degrees, NR), f32),
        ],
        compiler_params=params,
        name="solve",
    )(columns, operators)
    return advanced.reshape(3, 2, slots, degrees, NR)


def solution(mesh):
    in_specs = (
        P(None, None, "ma", "row", None),
        P(None, None, "ma", "row", None),
        P(),
        P("ma", None, None),
        P("ma", None, None),
        P("row", None, None),
    )
    out_specs = P(None, None, "ma", "row", None)
    return jax.shard_map(
        per_device, mesh=mesh, in_specs=in_specs, out_specs=out_specs, check_vma=False
    )
```

```python
import functools
import math

import jax
import jax.numpy as jnp
from jax import lax
from jax.experimental import pallas as pl
from jax.experimental.pallas import tpu as pltpu
from jax.sharding import PartitionSpec as P

NL = 384
NLAT = 576
NLON = 1152
NR = 128
LANES = 128


time_step = 0.5
rotation = 2.0

NT_DIMS = (((1,), (1,)), ((), ()))


def dot(left, right, dims=(((1,), (0,)), ((), ()))):
    return lax.dot_general(left, right, dims, preferred_element_type=jnp.float32)


def angle_parts(orders, steps):
    phases = orders[:, None] * steps[None, :] % NLON
    angles = phases.astype(jnp.float32) * (2.0 * math.pi / NLON)
    return jnp.cos(angles), jnp.sin(angles)


def tables_kernel(radii, coarse_cos, coarse_sin, fine_cos, fine_sin, operators, table, split):
    cos_b = fine_cos[...]
    sin_b = fine_sin[...]
    for block in range(NLON // LANES):
        cos_a = coarse_cos[:, block : block + 1]
        sin_a = coarse_sin[:, block : block + 1]
        lanes = pl.ds(block * LANES, LANES)
        table[:NL, lanes] = (cos_a * cos_b - sin_a * sin_b).astype(jnp.bfloat16)
        table[NL:, lanes] = (-(sin_a * cos_b + cos_a * sin_b)).astype(jnp.bfloat16)
    owners = NR // radii
    row = lax.broadcasted_iota(jnp.int32, (NR, NR), 0)
    column = lax.broadcasted_iota(jnp.int32, (NR, NR), 1)
    swap = (row == column % owners * radii + column // owners).astype(jnp.float32).astype(jnp.bfloat16)
    for degree in range(operators.shape[0]):
        operator = operators[degree]
        high = operator.astype(jnp.bfloat16)
        low = (operator - high.astype(jnp.float32)).astype(jnp.bfloat16)
        split[degree, :, :NR] = dot(high, swap).astype(jnp.bfloat16)
        split[degree, :, NR:] = dot(low, swap).astype(jnp.bfloat16)


def lane_index():
    return lax.broadcasted_iota(jnp.int32, (8, LANES), 1)


def joined(pieces, width, tile):
    start = tile * LANES
    lanes = lane_index()
    result = None
    for index in range(start // width, min(len(pieces), (start + LANES - 1) // width + 1)):
        offset = index * width - start
        moved = pieces[index]
        if offset % LANES:
            moved = pltpu.roll(moved, offset % LANES, 1)
        result = moved if result is None else jnp.where(lanes >= offset, moved, result)
    return result


def parted(tiles, width, index):
    tile, offset = divmod(index * width, LANES)
    piece = tiles[tile]
    if offset + width > LANES:
        piece = jnp.where(lane_index() >= offset, piece, tiles[tile + 1])
    if offset:
        piece = pltpu.roll(piece, LANES - offset, 1)
    return piece


def synthesis_kernel(
    groups,
    width,
    order_table,
    velocity,
    vorticity,
    legendre,
    out,
    orders,
    fields,
    tables,
    stage,
    turned,
    blocks,
    order_sem,
    field_sems,
    table_sems,
    block_sems,
):
    slots = tables.shape[0]
    radii = fields.shape[3]
    copies = [
        pltpu.make_async_copy(source, fields.at[index], field_sems.at[index])
        for index, source in enumerate((velocity, vorticity))
    ]
    loads = [
        pltpu.make_async_copy(legendre.at[slot, pl.ds(0, NLAT // 2)], tables.at[slot], table_sems.at[slot])
        for slot in range(slots)
    ]
    copies.append(pltpu.make_async_copy(order_table, orders, order_sem))
    for copy in copies + loads:
        copy.start()
    for copy in copies + loads:
        copy.wait()
    first = lax.axis_index("ma") * slots
    count = 12 * radii
    even = lax.broadcasted_iota(jnp.int32, (count, NL), 1) % 2 == 0
    for slot in range(slots):
        order = orders[first + slot]
        own = jnp.where(order == 0, 1.0, 2.0).astype(jnp.float32) / NL
        mirrored = jnp.where(order % 2 == 0, own, -own)
        spectral = fields[:, :, slot].astype(jnp.float32).reshape(count, NL)
        low = jnp.where(even, spectral, 0.0)
        both = jnp.concatenate([low, spectral - low], axis=0).astype(jnp.bfloat16)
        for group in range(groups // 2):
            sums = dot(both, tables[slot, group * width : (group + 1) * width, :], NT_DIMS)
            for hemisphere, part in enumerate(
                ((sums[:count] + sums[count:]) * own, (sums[:count] - sums[count:]) * mirrored)
            ):
                lane = (group + hemisphere * groups // 2) * LANES
                for field in range(12):
                    stage[field, slot * radii : (slot + 1) * radii, lane : lane + width] = part[
                        field * radii : (field + 1) * radii
                    ]
    count = slots * radii
    row = lax.broadcasted_iota(jnp.int32, (count, count), 0)
    column = lax.broadcasted_iota(jnp.int32, (count, count), 1)
    swap = (column == row % slots * radii + row // slots).astype(jnp.float32).astype(jnp.bfloat16)
    for field in range(12):
        turned[field] = dot(swap, stage[field].astype(jnp.bfloat16))
    stores = []
    for group in range(groups):
        for radius in range(radii):
            pieces = [
                turned[component * 2 + part, radius * slots : (radius + 1) * slots, group * LANES : (group + 1) * LANES]
                for part in range(2)
                for component in range(6)
            ]
            target = (group * radii + radius) * slots
            for tile in range(12 * width // LANES):
                blocks[target : target + slots, tile * LANES : (tile + 1) * LANES] = joined(
                    pieces, width, tile
                ).astype(jnp.bfloat16)
        rows = pl.ds(group * radii * slots, radii * slots)
        stores.append(pltpu.make_async_copy(blocks.at[rows], out.at[rows], block_sems.at[group]))
        stores[-1].start()
    for copy in stores:
        copy.wait()


def longitude_kernel(width, received, table, out, stage):
    points = 6 * width
    turned = received[...].astype(jnp.float32).T.astype(jnp.bfloat16)
    grid = dot(jnp.concatenate([turned[:points], turned[points:]], axis=1), table[...])
    u = [grid[c * width : (c + 1) * width] for c in range(3)]
    w = [grid[(3 + c) * width : (4 + c) * width] for c in range(3)]
    spin = w[2] + rotation
    products = jnp.concatenate(
        [
            u[1] * spin - u[2] * w[1],
            u[2] * w[0] - u[0] * spin,
            u[0] * w[1] - u[1] * w[0],
        ],
        axis=0,
    ).astype(jnp.bfloat16)
    back = (dot(products, table[...], NT_DIMS) * (NL / NLON)).T
    for part in range(2):
        stage[:, part * 3 * width : (part + 1) * 3 * width] = back[part * NL : (part + 1) * NL]
    out[...] = stage[...].astype(jnp.bfloat16)


def analysis_kernel(groups, width, orders, received, velocity, weighted, out, whole, side):
    slots = weighted.shape[0]
    radii = velocity.shape[2]
    tiles = whole.shape[0]
    for tile in range(tiles):
        size = min(LANES, 6 * width - tile * LANES)
        whole[tile, :, :size] = received[:, tile * LANES : tile * LANES + size].astype(jnp.float32)
    first = lax.axis_index("ma") * slots
    count = 6 * radii
    degree = lax.broadcasted_iota(jnp.int32, (count, NL), 1)
    for slot in range(slots):
        total = None
        for group in range(groups // 2):
            fields = []
            for block in (group, group + groups // 2):
                source = pl.ds(block * radii * slots + slot, radii, stride=slots)
                parts = [whole[tile, source, :] for tile in range(tiles)]
                fields += [parted(parts, width, part * 3 + component) for component in range(3) for part in range(2)]
            both = jnp.concatenate(fields, axis=0)[:, :width].astype(jnp.bfloat16)
            term = dot(both, weighted[slot, group * width : (group + 1) * width, :])
            total = term if total is None else total + term
        odd = (degree + orders[first + slot]) % 2 == 1
        terms = total[:count] + jnp.where(odd, -total[count:], total[count:])
        known = velocity[:, slot].astype(jnp.float32).reshape(6 * radii, NL)
        right_side = known + time_step * terms
        for field in range(6):
            for tile in range(NL // LANES):
                side[tile, pl.ds(field * slots + slot, radii, stride=6 * slots), :] = right_side[
                    field * radii : (field + 1) * radii, tile * LANES : (tile + 1) * LANES
                ]
    for tile in range(NL // LANES):
        out[tile * LANES : (tile + 1) * LANES, :] = side[tile].T.astype(jnp.bfloat16)


def solve_kernel(radii, received, operators, out, whole, results):
    degrees = operators.shape[0]
    owners = NR // radii
    count = received.shape[1] // radii
    tiles = whole.shape[0]
    for tile in range(tiles):
        whole[tile] = received[:, tile * LANES : (tile + 1) * LANES].astype(jnp.float32)
    for degree in range(degrees):
        halves = [
            [whole[tile, pl.ds(half * 8 * degrees + degree, 8, stride=degrees), :] for tile in range(tiles)]
            for half in range(owners // 8)
        ]
        pieces = [parted(parts, count, radius) for radius in range(radii) for parts in halves]
        columns = jnp.concatenate(pieces, axis=0).T[:count].astype(jnp.bfloat16)
        both = jnp.concatenate([columns, columns], axis=1)
        results[degree * count : (degree + 1) * count, :] = dot(both, operators[degree], NT_DIMS)
    for row in range(count):
        out[row * degrees : (row + 1) * degrees, :] = results[pl.ds(row, degrees, stride=count), :]


def per_device(velocity, vorticity, order_table, legendre_bf, weighted, inverse_operators):
    slots = velocity.shape[2]
    radii = velocity.shape[3]
    degrees = inverse_operators.shape[0]
    members = NL // slots
    owners = NL // degrees
    groups = members // radii
    width = NLAT // groups
    f32, bf16 = jnp.float32, jnp.bfloat16
    vmem = pl.BlockSpec(memory_space=pltpu.VMEM)
    params = pltpu.CompilerParams(vmem_limit_bytes=24 * 2**20)

    velocity_rows = velocity.reshape(6, slots, radii, NL)
    vorticity_rows = vorticity.reshape(6, slots, radii, NL)
    legendre_rows = jnp.swapaxes(legendre_bf, 1, 2)
    weighted_rows = jnp.swapaxes(weighted, 1, 2)

    hbm = pl.BlockSpec(memory_space=pl.ANY)
    sums = pl.pallas_call(
        functools.partial(synthesis_kernel, groups, width),
        in_specs=[hbm] * 4,
        out_specs=hbm,
        out_shape=jax.ShapeDtypeStruct((members * slots, 12 * width), bf16),
        scratch_shapes=[
            pltpu.SMEM((NL,), jnp.int32),
            pltpu.VMEM((2, 6, slots, radii, NL), bf16),
            pltpu.VMEM((slots, NLAT // 2, NL), bf16),
            pltpu.VMEM((12, slots * radii, groups * LANES), f32),
            pltpu.VMEM((12, slots * radii, groups * LANES), f32),
            pltpu.VMEM((members * slots, 12 * width), bf16),
            pltpu.SemaphoreType.DMA,
            pltpu.SemaphoreType.DMA((2,)),
            pltpu.SemaphoreType.DMA((slots,)),
            pltpu.SemaphoreType.DMA((groups,)),
        ],
        compiler_params=pltpu.CompilerParams(vmem_limit_bytes=60 * 2**20),
        name="synthesis",
    )(order_table, velocity_rows, vorticity_rows, legendre_rows)
    pieces = lax.all_to_all(
        sums.reshape(members, slots, 12 * width), "ma", split_axis=0, concat_axis=0, tiled=True
    ).reshape(members * slots, 12 * width)

    coarse_cos, coarse_sin = angle_parts(order_table, LANES * jnp.arange(LANES, dtype=jnp.int32) % NLON)
    fine_cos, fine_sin = angle_parts(order_table, jnp.arange(LANES, dtype=jnp.int32))
    table, operators = pl.pallas_call(
        functools.partial(tables_kernel, radii),
        in_specs=[vmem] * 5,
        out_specs=[vmem] * 2,
        out_shape=[
            jax.ShapeDtypeStruct((2 * NL, NLON), bf16),
            jax.ShapeDtypeStruct((degrees, NR, 2 * NR), bf16),
        ],
        cost_estimate=pl.CostEstimate(
            flops=6 * NL * NLON + 4 * degrees * NR**3,
            bytes_accessed=8 * NL * NLON + 8 * degrees * NR * NR,
            transcendentals=0,
        ),
        compiler_params=params,
        name="tables",
    )(coarse_cos, coarse_sin, fine_cos, fine_sin, inverse_operators)

    tendency = pl.pallas_call(
        functools.partial(longitude_kernel, width),
        in_specs=[vmem] * 2,
        out_specs=vmem,
        out_shape=jax.ShapeDtypeStruct((NL, 6 * width), bf16),
        scratch_shapes=[pltpu.VMEM((NL, 6 * width), f32)],
        compiler_params=params,
        name="longitude",
    )(pieces, table)
    pieces = lax.all_to_all(
        tendency.reshape(members, slots, 6 * width), "ma", split_axis=0, concat_axis=0, tiled=True
    ).reshape(members * slots, 6 * width)

    lanes = 6 * slots * radii
    sides = pl.pallas_call(
        functools.partial(analysis_kernel, groups, width),
        in_specs=[pl.BlockSpec(memory_space=pltpu.SMEM)] + [vmem] * 3,
        out_specs=vmem,
        out_shape=jax.ShapeDtypeStruct((NL, lanes), bf16),
        scratch_shapes=[
            pltpu.VMEM((pl.cdiv(6 * width, LANES), members * slots, LANES), f32),
            pltpu.VMEM((NL // LANES, lanes, LANES), f32),
        ],
        compiler_params=params,
        name="analysis",
    )(order_table, pieces, velocity_rows, weighted_rows)
    columns = lax.all_to_all(
        sides.reshape(owners, degrees, lanes), "row", split_axis=0, concat_axis=0, tiled=True
    ).reshape(NL, lanes)

    advanced = pl.pallas_call(
        functools.partial(solve_kernel, radii),
        in_specs=[vmem] * 2,
        out_specs=vmem,
        out_shape=jax.ShapeDtypeStruct((6 * slots * degrees, NR), f32),
        scratch_shapes=[
            pltpu.VMEM((lanes // LANES, NL, LANES), f32),
            pltpu.VMEM((6 * slots * degrees, NR), f32),
        ],
        compiler_params=params,
        name="solve",
    )(columns, operators)
    return advanced.reshape(3, 2, slots, degrees, NR)


def solution(mesh):
    in_specs = (
        P(None, None, "ma", "row", None),
        P(None, None, "ma", "row", None),
        P(),
        P("ma", None, None),
        P("ma", None, None),
        P("row", None, None),
    )
    out_specs = P(None, None, "ma", "row", None)
    return jax.shard_map(
        per_device, mesh=mesh, in_specs=in_specs, out_specs=out_specs, check_vma=False
    )
```

```python
import functools
import math

import jax
import jax.numpy as jnp
from jax import lax
from jax.experimental import pallas as pl
from jax.experimental.pallas import tpu as pltpu
from jax.sharding import PartitionSpec as P

NL = 384
NLAT = 576
NLON = 1152
NR = 128
LANES = 128


time_step = 0.5
rotation = 2.0

NT_DIMS = (((1,), (1,)), ((), ()))


def dot(left, right, dims=(((1,), (0,)), ((), ()))):
    return lax.dot_general(left, right, dims, preferred_element_type=jnp.float32)


def angle_parts(orders, steps):
    phases = orders[:, None] * steps[None, :] % NLON
    angles = phases.astype(jnp.float32) * (2.0 * math.pi / NLON)
    return jnp.cos(angles), jnp.sin(angles)


def tables_kernel(radii, coarse_cos, coarse_sin, fine_cos, fine_sin, operators, table, split):
    cos_b = fine_cos[...]
    sin_b = fine_sin[...]
    for block in range(NLON // LANES):
        cos_a = coarse_cos[:, block : block + 1]
        sin_a = coarse_sin[:, block : block + 1]
        lanes = pl.ds(block * LANES, LANES)
        table[:NL, lanes] = (cos_a * cos_b - sin_a * sin_b).astype(jnp.bfloat16)
        table[NL:, lanes] = (-(sin_a * cos_b + cos_a * sin_b)).astype(jnp.bfloat16)
    owners = NR // radii
    row = lax.broadcasted_iota(jnp.int32, (NR, NR), 0)
    column = lax.broadcasted_iota(jnp.int32, (NR, NR), 1)
    swap = (row == column % owners * radii + column // owners).astype(jnp.float32).astype(jnp.bfloat16)
    for degree in range(operators.shape[0]):
        operator = operators[degree]
        high = operator.astype(jnp.bfloat16)
        low = (operator - high.astype(jnp.float32)).astype(jnp.bfloat16)
        split[degree, :, :NR] = dot(high, swap).astype(jnp.bfloat16)
        split[degree, :, NR:] = dot(low, swap).astype(jnp.bfloat16)


def lane_index():
    return lax.broadcasted_iota(jnp.int32, (8, LANES), 1)


def joined(pieces, width, tile):
    start = tile * LANES
    lanes = lane_index()
    result = None
    for index in range(start // width, min(len(pieces), (start + LANES - 1) // width + 1)):
        offset = index * width - start
        moved = pieces[index]
        if offset % LANES:
            moved = pltpu.roll(moved, offset % LANES, 1)
        result = moved if result is None else jnp.where(lanes >= offset, moved, result)
    return result


def parted(tiles, width, index):
    tile, offset = divmod(index * width, LANES)
    piece = tiles[tile]
    if offset + width > LANES:
        piece = jnp.where(lane_index() >= offset, piece, tiles[tile + 1])
    if offset:
        piece = pltpu.roll(piece, LANES - offset, 1)
    return piece


def synthesis_kernel(
    groups,
    width,
    order_table,
    velocity,
    vorticity,
    legendre,
    out,
    orders,
    fields,
    tables,
    stage,
    turned,
    blocks,
    order_sem,
    field_sems,
    table_sems,
    block_sems,
):
    slots = tables.shape[0]
    radii = fields.shape[3]
    copies = [
        pltpu.make_async_copy(source, fields.at[index], field_sems.at[index])
        for index, source in enumerate((velocity, vorticity))
    ]
    loads = [
        pltpu.make_async_copy(legendre.at[slot, pl.ds(0, NLAT // 2)], tables.at[slot], table_sems.at[slot])
        for slot in range(slots)
    ]
    copies.append(pltpu.make_async_copy(order_table, orders, order_sem))
    for copy in copies + loads:
        copy.start()
    for copy in copies + loads:
        copy.wait()
    first = lax.axis_index("ma") * slots
    count = 12 * radii
    even = lax.broadcasted_iota(jnp.int32, (count, NL), 1) % 2 == 0
    for slot in range(slots):
        order = orders[first + slot]
        own = jnp.where(order == 0, 1.0, 2.0).astype(jnp.float32) / NL
        mirrored = jnp.where(order % 2 == 0, own, -own)
        spectral = fields[:, :, slot].astype(jnp.float32).reshape(count, NL)
        low = jnp.where(even, spectral, 0.0)
        both = jnp.concatenate([low, spectral - low], axis=0).astype(jnp.bfloat16)
        for group in range(groups // 2):
            sums = dot(both, tables[slot, group * width : (group + 1) * width, :], NT_DIMS)
            for hemisphere, part in enumerate(
                ((sums[:count] + sums[count:]) * own, (sums[:count] - sums[count:]) * mirrored)
            ):
                lane = (group + hemisphere * groups // 2) * LANES
                for field in range(12):
                    stage[field, slot * radii : (slot + 1) * radii, lane : lane + width] = part[
                        field * radii : (field + 1) * radii
                    ]
    count = slots * radii
    row = lax.broadcasted_iota(jnp.int32, (count, count), 0)
    column = lax.broadcasted_iota(jnp.int32, (count, count), 1)
    swap = (column == row % slots * radii + row // slots).astype(jnp.float32).astype(jnp.bfloat16)
    for field in range(12):
        turned[field] = dot(swap, stage[field].astype(jnp.bfloat16))
    stores = []
    for group in range(groups):
        for radius in range(radii):
            pieces = [
                turned[component * 2 + part, radius * slots : (radius + 1) * slots, group * LANES : (group + 1) * LANES]
                for part in range(2)
                for component in range(6)
            ]
            target = (group * radii + radius) * slots
            for tile in range(12 * width // LANES):
                blocks[target : target + slots, tile * LANES : (tile + 1) * LANES] = joined(
                    pieces, width, tile
                ).astype(jnp.bfloat16)
        rows = pl.ds(group * radii * slots, radii * slots)
        stores.append(pltpu.make_async_copy(blocks.at[rows], out.at[rows], block_sems.at[group]))
        stores[-1].start()
    for copy in stores:
        copy.wait()


def longitude_kernel(width, received, table, out, stage):
    points = 6 * width
    turned = received[...].astype(jnp.float32).T.astype(jnp.bfloat16)
    grid = dot(jnp.concatenate([turned[:points], turned[points:]], axis=1), table[...])
    u = [grid[c * width : (c + 1) * width] for c in range(3)]
    w = [grid[(3 + c) * width : (4 + c) * width] for c in range(3)]
    spin = w[2] + rotation
    products = jnp.concatenate(
        [
            u[1] * spin - u[2] * w[1],
            u[2] * w[0] - u[0] * spin,
            u[0] * w[1] - u[1] * w[0],
        ],
        axis=0,
    ).astype(jnp.bfloat16)
    back = (dot(products, table[...], NT_DIMS) * (NL / NLON)).T
    for part in range(2):
        stage[:, part * 3 * width : (part + 1) * 3 * width] = back[part * NL : (part + 1) * NL]
    out[...] = stage[...].astype(jnp.bfloat16)


def analysis_kernel(groups, width, signs, received, velocity, weighted, out, whole, side):
    slots = weighted.shape[0]
    radii = velocity.shape[2]
    tiles = whole.shape[0]
    for tile in range(tiles):
        size = min(LANES, 6 * width - tile * LANES)
        whole[tile, :, :size] = received[:, tile * LANES : tile * LANES + size].astype(jnp.float32)
    count = 6 * radii
    for slot in range(slots):
        total = None
        for group in range(groups // 2):
            fields = []
            for block in (group, group + groups // 2):
                source = pl.ds(block * radii * slots + slot, radii, stride=slots)
                parts = [whole[tile, source, :] for tile in range(tiles)]
                fields += [parted(parts, width, part * 3 + component) for component in range(3) for part in range(2)]
            both = jnp.concatenate(fields, axis=0)[:, :width].astype(jnp.bfloat16)
            term = dot(both, weighted[slot, group * width : (group + 1) * width, :])
            total = term if total is None else total + term
        terms = total[:count] + total[count:] * signs[slot : slot + 1, :]
        known = velocity[:, slot].astype(jnp.float32).reshape(6 * radii, NL)
        right_side = known + time_step * terms
        for field in range(6):
            for tile in range(NL // LANES):
                side[tile, pl.ds(field * slots + slot, radii, stride=6 * slots), :] = right_side[
                    field * radii : (field + 1) * radii, tile * LANES : (tile + 1) * LANES
                ]
    for tile in range(NL // LANES):
        out[tile * LANES : (tile + 1) * LANES, :] = side[tile].T.astype(jnp.bfloat16)


def solve_kernel(radii, received, operators, out, whole, results):
    degrees = operators.shape[0]
    owners = NR // radii
    count = received.shape[1] // radii
    tiles = whole.shape[0]
    for tile in range(tiles):
        whole[tile] = received[:, tile * LANES : (tile + 1) * LANES].astype(jnp.float32)
    for degree in range(degrees):
        halves = [
            [whole[tile, pl.ds(half * 8 * degrees + degree, 8, stride=degrees), :] for tile in range(tiles)]
            for half in range(owners // 8)
        ]
        pieces = [parted(parts, count, radius) for radius in range(radii) for parts in halves]
        columns = jnp.concatenate(pieces, axis=0).T[:count].astype(jnp.bfloat16)
        both = jnp.concatenate([columns, columns], axis=1)
        results[degree * count : (degree + 1) * count, :] = dot(both, operators[degree], NT_DIMS)
    for row in range(count):
        out[row * degrees : (row + 1) * degrees, :] = results[pl.ds(row, degrees, stride=count), :]


def per_device(velocity, vorticity, order_table, legendre_bf, weighted, inverse_operators):
    slots = velocity.shape[2]
    radii = velocity.shape[3]
    degrees = inverse_operators.shape[0]
    members = NL // slots
    owners = NL // degrees
    groups = members // radii
    width = NLAT // groups
    f32, bf16 = jnp.float32, jnp.bfloat16
    vmem = pl.BlockSpec(memory_space=pltpu.VMEM)
    params = pltpu.CompilerParams(vmem_limit_bytes=24 * 2**20)

    velocity_rows = velocity.reshape(6, slots, radii, NL)
    vorticity_rows = vorticity.reshape(6, slots, radii, NL)
    legendre_rows = jnp.swapaxes(legendre_bf, 1, 2)
    weighted_rows = jnp.swapaxes(weighted, 1, 2)

    hbm = pl.BlockSpec(memory_space=pl.ANY)
    sums = pl.pallas_call(
        functools.partial(synthesis_kernel, groups, width),
        in_specs=[hbm] * 4,
        out_specs=hbm,
        out_shape=jax.ShapeDtypeStruct((members * slots, 12 * width), bf16),
        scratch_shapes=[
            pltpu.SMEM((NL,), jnp.int32),
            pltpu.VMEM((2, 6, slots, radii, NL), bf16),
            pltpu.VMEM((slots, NLAT // 2, NL), bf16),
            pltpu.VMEM((12, slots * radii, groups * LANES), f32),
            pltpu.VMEM((12, slots * radii, groups * LANES), f32),
            pltpu.VMEM((members * slots, 12 * width), bf16),
            pltpu.SemaphoreType.DMA,
            pltpu.SemaphoreType.DMA((2,)),
            pltpu.SemaphoreType.DMA((slots,)),
            pltpu.SemaphoreType.DMA((groups,)),
        ],
        compiler_params=pltpu.CompilerParams(vmem_limit_bytes=60 * 2**20),
        name="synthesis",
    )(order_table, velocity_rows, vorticity_rows, legendre_rows)
    pieces = lax.all_to_all(
        sums.reshape(members, slots, 12 * width), "ma", split_axis=0, concat_axis=0, tiled=True
    ).reshape(members * slots, 12 * width)

    coarse_cos, coarse_sin = angle_parts(order_table, LANES * jnp.arange(LANES, dtype=jnp.int32) % NLON)
    fine_cos, fine_sin = angle_parts(order_table, jnp.arange(LANES, dtype=jnp.int32))
    table, operators = pl.pallas_call(
        functools.partial(tables_kernel, radii),
        in_specs=[vmem] * 5,
        out_specs=[vmem] * 2,
        out_shape=[
            jax.ShapeDtypeStruct((2 * NL, NLON), bf16),
            jax.ShapeDtypeStruct((degrees, NR, 2 * NR), bf16),
        ],
        cost_estimate=pl.CostEstimate(
            flops=6 * NL * NLON + 4 * degrees * NR**3,
            bytes_accessed=8 * NL * NLON + 8 * degrees * NR * NR,
            transcendentals=0,
        ),
        compiler_params=params,
        name="tables",
    )(coarse_cos, coarse_sin, fine_cos, fine_sin, inverse_operators)

    own_orders = lax.dynamic_slice_in_dim(order_table, lax.axis_index("ma") * slots, slots)
    parity = (own_orders[:, None] + jnp.arange(NL, dtype=jnp.int32)[None, :]) % 2
    signs = (1 - 2 * parity).astype(f32)
    table, signs = lax.optimization_barrier((table, signs))

    tendency = pl.pallas_call(
        functools.partial(longitude_kernel, width),
        in_specs=[vmem] * 2,
        out_specs=vmem,
        out_shape=jax.ShapeDtypeStruct((NL, 6 * width), bf16),
        scratch_shapes=[pltpu.VMEM((NL, 6 * width), f32)],
        compiler_params=params,
        name="longitude",
    )(pieces, table)
    pieces = lax.all_to_all(
        tendency.reshape(members, slots, 6 * width), "ma", split_axis=0, concat_axis=0, tiled=True
    ).reshape(members * slots, 6 * width)

    lanes = 6 * slots * radii
    sides = pl.pallas_call(
        functools.partial(analysis_kernel, groups, width),
        in_specs=[vmem] * 4,
        out_specs=vmem,
        out_shape=jax.ShapeDtypeStruct((NL, lanes), bf16),
        scratch_shapes=[
            pltpu.VMEM((pl.cdiv(6 * width, LANES), members * slots, LANES), f32),
            pltpu.VMEM((NL // LANES, lanes, LANES), f32),
        ],
        compiler_params=params,
        name="analysis",
    )(signs, pieces, velocity_rows, weighted_rows)
    columns = lax.all_to_all(
        sides.reshape(owners, degrees, lanes), "row", split_axis=0, concat_axis=0, tiled=True
    ).reshape(NL, lanes)

    advanced = pl.pallas_call(
        functools.partial(solve_kernel, radii),
        in_specs=[vmem] * 2,
        out_specs=vmem,
        out_shape=jax.ShapeDtypeStruct((6 * slots * degrees, NR), f32),
        scratch_shapes=[
            pltpu.VMEM((lanes // LANES, NL, LANES), f32),
            pltpu.VMEM((6 * slots * degrees, NR), f32),
        ],
        compiler_params=params,
        name="solve",
    )(columns, operators)
    return advanced.reshape(3, 2, slots, degrees, NR)


def solution(mesh):
    in_specs = (
        P(None, None, "ma", "row", None),
        P(None, None, "ma", "row", None),
        P(),
        P("ma", None, None),
        P("ma", None, None),
        P("row", None, None),
    )
    out_specs = P(None, None, "ma", "row", None)
    return jax.shard_map(
        per_device, mesh=mesh, in_specs=in_specs, out_specs=out_specs, check_vma=False
    )
```
